32 devices in a mesh: visit: 4 (over z), patch: 8 (over y, x, core).
Axes of the slice: x: 2, y: 2, z: 4, core: 2. Of those that a mesh axis runs over, the one named last changes fastest.
Arguments:
- warped_tiles: bfloat16 [1024, 256, 256], P(('visit', 'patch')), may hold values from -6 to 6
- tile_weights: bfloat16 [1024], P(('visit', 'patch')), may hold values from 1 to 9984
- kernel_taps: bfloat16 [1024, 2, 15], P(('visit', 'patch')), may hold values from -3 to 3
- patch_routes: int32 [1024, 1], P(('visit', 'patch')), may hold values from 0 to 7; in each aligned block of 32 rows (0 to 31, 32 to 63, ...) at most 8 rows name the same one
Outputs:
- difference: bfloat16 [1024, 256, 256], P(('visit', 'patch'))
- coadd_image: bfloat16 [8, 256, 256], P('patch')
The draws below stay inside these ranges and needn't reach their ends.
Inputs may be any that keep to these rules, and one draw needn't show every extreme that they name: `patch_routes`: among the 32 rows of one device no patch is named more than 8 times, a bound that some block reaches; every patch is named by some row.
All inputs are finite; a program needn't handle non-finite values.
Results may differ from the reference program's by a relative error of at most 0.0046.
Values may be sent and summed in bfloat16 or wider, within the bound.
A program may use at most 128 MiB of HBM per device.

```python
import math
import jax
import jax.numpy as jnp
import numpy as np
from jax import lax

TILE = 256
KERNEL = 15
TILE_DEV = 32
SLOT_CAP = 8
PATCHES = 8
TILES = 1024


def level_of(rng, dims, split, low, largest):
    level, own = 1.0, jax.random.fold_in(rng, 6)
    for position, parts in split:
        draws = jnp.exp(jax.random.uniform(jax.random.fold_in(own, position), (parts,), jnp.float32, low / len(split), largest / len(split)))
        level = level * jnp.repeat(draws, dims[position] // parts).reshape([-1 if axis == position else 1 for axis in range(len(dims))])
    return level


def routed_block(rng, own, number, rows, amount, top, most, lean):
    order = jax.random.permutation(rng, amount)
    heavy_load, usual = portions_of(amount, rows * top, most, lean, True), portions_of(amount, rows * top, most, lean, False)
    places = jnp.arange(amount)

    def named(sizes, rotation):
        used = int((sizes > 0).sum())
        fixed = max(1, used // 4)
        passed = fixed + (places - fixed + rotation * (used - fixed)) % max(1, amount - fixed)
        return jnp.zeros((amount,), jnp.int32).at[order[jnp.where(places < fixed, places, passed)]].set(jnp.asarray(sizes, jnp.int32))

    sizes = jnp.where(number % 4 == 0, named(heavy_load, number // 4), named(usual, number - number // 4 - 1))
    mixed = jax.random.permutation(jax.random.fold_in(own, 3), amount)
    source_of, taker = mixed[0:amount // 2 * 2:2], mixed[1:amount // 2 * 2:2]
    margin = jnp.minimum(sizes[source_of] - 1, most - sizes[taker]) // 2
    margin = jnp.where((source_of == order[0]) | (taker == order[0]) | (sizes[taker] == 0), 0, jnp.maximum(margin, 0))
    passed = jax.random.randint(jax.random.fold_in(own, 4), (amount // 2,), 0, 1 << 20) % (margin + 1)
    sizes = sizes.at[source_of].add(-passed).at[taker].add(passed)
    members = jnp.searchsorted(jnp.cumsum(sizes), jnp.arange(rows * top), side="right").astype(jnp.int32)
    grid = members.reshape(top, rows).T
    grid = grid[jax.random.permutation(jax.random.fold_in(own, 1), rows)]
    rotation = jax.random.randint(jax.random.fold_in(own, 2), (rows, 1), 0, top)
    return jnp.take_along_axis(grid, (jnp.arange(top)[None, :] + rotation) % top, axis=1)


def portions_of(amount, total, bound, lean, full):
    portions = [(1 << 20) // math.isqrt(grade ** lean) + 1 for grade in range(1, amount + 1)]
    largest = bound if full else min(bound, max(-(-total // amount), total * portions[0] // sum(portions)))
    least = 1 if total - largest >= amount - 1 else 0
    holding, rest = [largest] + [least] * (amount - 1), total - largest - least * (amount - 1)
    while rest > 0:
        movable = [i for i in range(1, amount) if holding[i] < largest] or [i for i in range(1, amount) if holding[i] < bound]
        pool, remaining = sum([portions[i] for i in movable]), rest
        for i in movable:
            extra = min(bound - holding[i], max(1, remaining * portions[i] // pool), rest)
            holding[i] = holding[i] + extra
            rest = rest - extra
    return np.array(holding)


def centred(key, shape, width, limit, split=(), kind=jnp.bfloat16):
    drawn = jax.random.normal(key, shape, jnp.float32) * width
    if len(split) > 0:
        drawn = level_of(key, shape, split, -0.22, 0.18) * drawn
    return jnp.clip(drawn, min=-limit, max=limit).astype(kind)


def setup_inputs(seed: int = 0) -> dict:
    key_of = jax.random.split(jax.random.key(seed), 5)
    warped_tiles = centred(key_of[0], (TILES, TILE, TILE), 1.0, 6.0, ((0, 32),))
    tile_weights = jnp.clip(jnp.exp(math.log(9984.0) - 9.208739 * jax.random.uniform(key_of[1], (TILES,), jnp.float32) ** level_of(key_of[1], (TILES,), ((0, 32),), -0.2, 0.2)), 1.0, 9984.0).astype(jnp.bfloat16)
    kernel_taps = centred(key_of[2], (TILES, 2, KERNEL), 0.4, 3.0, ((0, 32),))
    patch_routes_keys = jax.random.split(jax.random.fold_in(key_of[3], 1), TILES // TILE_DEV)
    patch_routes_turns = jax.random.permutation(jax.random.fold_in(key_of[3], 3), TILES // TILE_DEV)
    patch_routes = jax.vmap(lambda own, number: routed_block(jax.random.fold_in(key_of[3], 2), own, number, TILE_DEV, PATCHES, 1, SLOT_CAP, 2))(patch_routes_keys, patch_routes_turns).reshape((TILES, 1))
    return dict(warped_tiles=warped_tiles, tile_weights=tile_weights, kernel_taps=kernel_taps, patch_routes=patch_routes)


def shift_table(tile_side, kernel):
    rows = jnp.arange(tile_side, dtype=jnp.int32)
    offsets = (rows[None, :] - rows[:, None] + kernel // 2).reshape(-1)
    return (offsets[None, :] == jnp.arange(kernel, dtype=jnp.int32)[:, None]).astype(jnp.bfloat16)


def banded(taps_rows, table, tile_side):
    flat = jnp.dot(taps_rows, table, preferred_element_type=jnp.float32).astype(jnp.bfloat16)
    return flat.reshape(taps_rows.shape[0], tile_side, tile_side)


def match_psf(taps_block, coadd_block, table, tile_side):
    row_bands = banded(taps_block[:, 0, :], table, tile_side)
    col_bands = banded(taps_block[:, 1, :], table, tile_side)
    row_pass = jnp.einsum("nij,njk->nik", row_bands.astype(jnp.float32), coadd_block.astype(jnp.float32)).astype(jnp.bfloat16)
    return jnp.einsum("nik,nlk->nil", row_pass.astype(jnp.float32), col_bands.astype(jnp.float32)).astype(jnp.bfloat16)


def reference(warped_tiles, tile_weights, kernel_taps, patch_routes):
    target = patch_routes[:, 0]
    route_hot = jnp.arange(PATCHES, dtype=jnp.int32)[:, None] == target[None, :]
    weighted_hot = jnp.where(route_hot, tile_weights[None, :], jnp.zeros((), jnp.bfloat16))
    coadd_sum = jnp.dot(weighted_hot, warped_tiles.reshape(TILES, TILE * TILE), preferred_element_type=jnp.float32)
    weight_total = jnp.sum(jnp.where(route_hot, tile_weights[None, :].astype(jnp.float32), jnp.float32(0.0)), axis=1)
    coadd_image = (coadd_sum / weight_total[:, None]).astype(jnp.bfloat16).reshape(PATCHES, TILE, TILE)
    table = shift_table(TILE, KERNEL)
    blocks = TILES // TILE_DEV

    def one_block(packed):
        tile_block, taps_block, target_block = packed
        chosen = coadd_image[target_block]
        template = match_psf(taps_block, chosen, table, TILE)
        return (tile_block.astype(jnp.float32) - template.astype(jnp.float32)).astype(jnp.bfloat16)

    difference = lax.map(one_block, (warped_tiles.reshape(blocks, TILE_DEV, TILE, TILE), kernel_taps.reshape(blocks, TILE_DEV, 2, KERNEL), target.reshape(blocks, TILE_DEV)))
    return difference.reshape(TILES, TILE, TILE), coadd_image
```

```python
import functools
import jax
import jax.numpy as jnp
from jax import lax
from jax.experimental import pallas as pl
from jax.experimental.pallas import tpu as pltpu
from jax.sharding import PartitionSpec as P


def sum_kernel(patches, routes, weights, tiles, part, totals, acc):
    acc[...] = jnp.zeros_like(acc)
    for t in range(tiles.shape[0]):
        acc[routes[t]] += tiles[t].astype(jnp.float32) * weights[t]
    part[...] = acc[...].astype(part.dtype)

    @pl.when(pl.program_id(0) == 0)
    def _():
        totals[...] = jnp.zeros_like(totals)
        for t in range(tiles.shape[0]):
            totals[routes[t]] += jnp.full(totals.shape[1:], weights[t], jnp.float32)


def local_sums(tiles, weights, routes, patches, chunk, dtype):
    count, side, _ = tiles.shape
    return pl.pallas_call(
        functools.partial(sum_kernel, patches),
        grid_spec=pltpu.PrefetchScalarGridSpec(
            num_scalar_prefetch=2,
            grid=(side // chunk,),
            in_specs=[pl.BlockSpec((count, chunk, side), lambda i, *_: (0, i, 0))],
            out_specs=[
                pl.BlockSpec((patches, chunk, side), lambda i, *_: (0, i, 0)),
                pl.BlockSpec((patches, 8, 128), lambda i, *_: (0, 0, 0)),
            ],
            scratch_shapes=[pltpu.VMEM((patches, chunk, side), jnp.float32)],
        ),
        out_shape=[
            jax.ShapeDtypeStruct((patches, side, side), dtype),
            jax.ShapeDtypeStruct((patches, 8, 128), jnp.float32),
        ],
        name="local_sums",
    )(routes, weights, tiles)


def band(row):
    half = 128
    ring = pltpu.roll(jnp.broadcast_to(row, (half, half)), 0, 1, stride=1, stride_axis=0)
    gap = lax.broadcasted_iota(jnp.int32, (half, half), 1) - lax.broadcasted_iota(jnp.int32, (half, half), 0)
    zero = jnp.zeros_like(ring)
    near = jnp.where((gap < 64) & (gap > -64), ring, zero).astype(jnp.bfloat16)
    upper = jnp.where(gap <= -64, ring, zero).astype(jnp.bfloat16)
    lower = jnp.where(gap >= 64, ring, zero).astype(jnp.bfloat16)
    return jnp.concatenate(
        [jnp.concatenate([near, upper], axis=1), jnp.concatenate([lower, near], axis=1)], axis=0
    )


def match_kernel(routes, taps, tiles, coadd, out):
    step = pl.program_id(0)
    group = tiles.shape[0]
    for g in range(group):
        image = coadd[routes[step * group + g]]
        row_pass = jnp.dot(band(taps[g, 0:1, :]), image, preferred_element_type=jnp.float32).astype(jnp.bfloat16)
        template = jnp.dot(row_pass, band(taps[g, 1:2, :]), preferred_element_type=jnp.float32).astype(jnp.bfloat16)
        out[g] = (tiles[g].astype(jnp.float32) - template.astype(jnp.float32)).astype(out.dtype)


def subtract(tiles, rings, routes, coadd, group):
    count, side, _ = tiles.shape
    return pl.pallas_call(
        match_kernel,
        grid_spec=pltpu.PrefetchScalarGridSpec(
            num_scalar_prefetch=1,
            grid=(count // group,),
            in_specs=[
                pl.BlockSpec((group, 2, 128), lambda i, *_: (i, 0, 0)),
                pl.BlockSpec((group, side, side), lambda i, *_: (i, 0, 0)),
                pl.BlockSpec(coadd.shape, lambda i, *_: (0, 0, 0)),
            ],
            out_specs=pl.BlockSpec((group, side, side), lambda i, *_: (i, 0, 0)),
        ),
        out_shape=jax.ShapeDtypeStruct(tiles.shape, jnp.bfloat16),
        name="subtract",
    )(routes, rings, tiles, coadd)


def ring_rows(taps):
    count, _, kernel = taps.shape
    both = jnp.stack([taps[:, 0, :], taps[:, 1, ::-1]], axis=1).astype(jnp.float32)
    reach = kernel // 2
    gap = jnp.zeros((count, 2, 128 - kernel), jnp.float32)
    return jnp.concatenate([both[:, :, reach:], gap, both[:, :, :reach]], axis=2)


def local(warped_tiles, tile_weights, kernel_taps, patch_routes):
    patches = lax.axis_size("patch")
    side = warped_tiles.shape[1]
    routes = patch_routes[:, 0]
    weights = tile_weights.astype(jnp.float32)
    rings = ring_rows(kernel_taps)
    part, totals = local_sums(warped_tiles, weights, routes, patches, 64, jnp.float32)
    total = lax.psum(totals, ("visit", "patch"))
    mine = lax.psum_scatter(part, "patch", scatter_dimension=0, tiled=True)
    mine = lax.psum(mine, "visit")[0]
    own_total = lax.dynamic_index_in_dim(total, lax.axis_index("patch"), 0, keepdims=False)[0, 0]
    coadd_image = (mine / own_total).astype(jnp.bfloat16)[None]
    coadd = lax.all_gather(coadd_image, "patch", axis=0, tiled=True)
    difference = subtract(warped_tiles, rings, routes, coadd, 4)
    return (difference, coadd_image)


def solution(mesh):
    in_specs = (
        P(("visit", "patch"), None, None),
        P(("visit", "patch")),
        P(("visit", "patch"), None, None),
        P(("visit", "patch"), None),
    )
    out_specs = (P(("visit", "patch"), None, None), P("patch", None, None))
    return jax.shard_map(local, mesh=mesh, in_specs=in_specs, out_specs=out_specs, check_vma=False)
```

```python
import functools
import jax
import jax.numpy as jnp
from jax import lax
from jax.experimental import pallas as pl
from jax.experimental.pallas import tpu as pltpu
from jax.sharding import PartitionSpec as P


def sum_kernel(patches, routes, weights, tiles, part, totals, acc):
    acc[...] = jnp.zeros_like(acc)
    for t in range(tiles.shape[0]):
        acc[routes[t]] += tiles[t].astype(jnp.float32) * weights[t]
    part[...] = acc[...].astype(part.dtype)

    @pl.when(pl.program_id(0) == 0)
    def _():
        totals[...] = jnp.zeros_like(totals)
        for t in range(tiles.shape[0]):
            totals[routes[t]] += jnp.full(totals.shape[1:], weights[t], jnp.float32)


def local_sums(tiles, weights, routes, patches, chunk, dtype):
    count, side, _ = tiles.shape
    return pl.pallas_call(
        functools.partial(sum_kernel, patches),
        grid_spec=pltpu.PrefetchScalarGridSpec(
            num_scalar_prefetch=2,
            grid=(side // chunk,),
            in_specs=[pl.BlockSpec((count, chunk, side), lambda i, *_: (0, i, 0))],
            out_specs=[
                pl.BlockSpec((patches, chunk, side), lambda i, *_: (0, i, 0)),
                pl.BlockSpec((patches, 8, 128), lambda i, *_: (0, 0, 0)),
            ],
            scratch_shapes=[pltpu.VMEM((patches, chunk, side), jnp.float32)],
        ),
        out_shape=[
            jax.ShapeDtypeStruct((patches, side, side), dtype),
            jax.ShapeDtypeStruct((patches, 8, 128), jnp.float32),
        ],
        name="local_sums",
    )(routes, weights, tiles)


def band(row):
    half = 128
    ring = pltpu.roll(jnp.broadcast_to(row, (half, half)), 0, 1, stride=1, stride_axis=0)
    gap = lax.broadcasted_iota(jnp.int32, (half, half), 1) - lax.broadcasted_iota(jnp.int32, (half, half), 0)
    zero = jnp.zeros_like(ring)
    near = jnp.where((gap < 64) & (gap > -64), ring, zero).astype(jnp.bfloat16)
    upper = jnp.where(gap <= -64, ring, zero).astype(jnp.bfloat16)
    lower = jnp.where(gap >= 64, ring, zero).astype(jnp.bfloat16)
    return jnp.concatenate(
        [jnp.concatenate([near, upper], axis=1), jnp.concatenate([lower, near], axis=1)], axis=0
    )


def match_kernel(routes, taps, tiles, coadd, out):
    step = pl.program_id(0)
    group = tiles.shape[0]
    for g in range(group):
        image = coadd[routes[step * group + g]]
        row_pass = jnp.dot(band(taps[g, 0:1, :]), image, preferred_element_type=jnp.float32).astype(jnp.bfloat16)
        template = jnp.dot(row_pass, band(taps[g, 1:2, :]), preferred_element_type=jnp.float32).astype(jnp.bfloat16)
        out[g] = (tiles[g].astype(jnp.float32) - template.astype(jnp.float32)).astype(out.dtype)


def subtract(tiles, rings, routes, coadd, group):
    count, side, _ = tiles.shape
    return pl.pallas_call(
        match_kernel,
        grid_spec=pltpu.PrefetchScalarGridSpec(
            num_scalar_prefetch=1,
            grid=(count // group,),
            in_specs=[
                pl.BlockSpec((group, 2, 128), lambda i, *_: (i, 0, 0)),
                pl.BlockSpec((group, side, side), lambda i, *_: (i, 0, 0)),
                pl.BlockSpec(coadd.shape, lambda i, *_: (0, 0, 0)),
            ],
            out_specs=pl.BlockSpec((group, side, side), lambda i, *_: (i, 0, 0)),
        ),
        out_shape=jax.ShapeDtypeStruct(tiles.shape, jnp.bfloat16),
        name="subtract",
    )(routes, rings, tiles, coadd)


def ring_rows(taps):
    count, _, kernel = taps.shape
    both = jnp.stack([taps[:, 0, :], taps[:, 1, ::-1]], axis=1).astype(jnp.float32)
    reach = kernel // 2
    gap = jnp.zeros((count, 2, 128 - kernel), jnp.float32)
    return jnp.concatenate([both[:, :, reach:], gap, both[:, :, :reach]], axis=2)


def merge_kernel(chips, visits, part, totals, coadd, own, half, chip_sum, inbox, lane_sum, lane_in, mine,
                 tot_in, tot_mid, tot_z, core_s, core_r, chip_s, chip_r, lane_s, lane_r,
                 back_s, back_r, fan_s, fan_r, pair_s, pair_r, tot_s, tot_r, totz_s, totz_r):
    v = lax.axis_index("visit")
    p = lax.axis_index("patch")
    k, c = p // 2, p % 2
    patches = 2 * chips
    side = part.shape[2]
    rows = side // visits
    sibling = 2 * k + 1 - c

    def span(r):
        return pl.ds(pl.multiple_of(r * rows, rows), rows)

    def remote(src, dst, send, recv, visit, patch):
        return pltpu.make_async_remote_copy(
            src_ref=src, dst_ref=dst, send_sem=send, recv_sem=recv,
            device_id=(visit, patch), device_id_type=pl.DeviceIdType.MESH)

    def chip_at(o):
        return lax.rem(k + o, chips)

    def visit_at(o):
        return lax.rem(v + o, visits)

    def loop(low, high, body):
        if (high - low) <= 4:
            for i in range(low, high):
                body(i)
        else:
            lax.fori_loop(low, high, lambda i, _: (body(i), 0)[1], 0)

    def core_copy(j, r):
        return remote(part.at[j, 1 - c, span(r)], half.at[j, span(r)], core_s.at[j, r], core_r.at[j, r], v, sibling)

    def chip_copy(j, slot, r):
        return remote(chip_sum.at[j, span(r)], inbox.at[slot, span(r)], chip_s.at[j, r], chip_r.at[slot, r], v, 2 * j + c)

    def lane_copy(u, slot):
        return remote(lane_sum.at[u], lane_in.at[slot], lane_s.at[u], lane_r.at[slot], u, p)

    def tot_copy(q, slot):
        return remote(totals.at[q], tot_in.at[slot], tot_s.at[q], tot_r.at[slot], v, q)

    def totz_copy(u, slot):
        return remote(tot_mid, tot_z.at[slot], totz_s.at[u], totz_r.at[slot], u, p)

    def back_copy(u, r):
        piece = coadd.at[p, span(r)]
        return remote(piece, piece, back_s.at[u], back_r.at[r], u, p)

    def fan_copy(j, slot, r):
        piece = coadd.at[2 * slot + c, span(r)]
        return remote(piece, piece, fan_s.at[j, r], fan_r.at[slot, r], v, 2 * j + c)

    def pair_copy(j, core, r):
        piece = coadd.at[2 * j + core, span(r)]
        return remote(piece, piece, pair_s.at[j, r], pair_r.at[j, r], v, sibling)

    barrier = pltpu.get_barrier_semaphore()

    def greet_patch(o):
        pl.semaphore_signal(barrier, inc=1, device_id=(v, lax.rem(p + o, patches)), device_id_type=pl.DeviceIdType.MESH)

    def greet_visit(o):
        pl.semaphore_signal(barrier, inc=1, device_id=(visit_at(o), p), device_id_type=pl.DeviceIdType.MESH)

    loop(1, patches, greet_patch)
    loop(1, visits, greet_visit)
    pl.semaphore_wait(barrier, patches - 1 + visits - 1)

    def start_core(i):
        r = visit_at(i + 1)
        loop(1, chips + 1, lambda o: core_copy(chip_at(o), r).start())

    loop(0, visits, start_core)

    def start_tot(o):
        tot_copy(lax.rem(p + o, patches), p).start()

    loop(1, patches, start_tot)

    def send_chips(i):
        r = visit_at(i + 1)

        def one(o):
            j = chip_at(o)
            core_copy(j, r).wait_recv()
            chip_sum[j, span(r)] = (
                part[j, c, span(r)].astype(jnp.float32) + half[j, span(r)].astype(jnp.float32)
            ).astype(jnp.bfloat16)
            chip_copy(j, k, r).start()

        loop(1, chips, one)

    loop(0, visits, send_chips)

    tot_mid[...] = totals[p]

    def add_tot(o):
        q = lax.rem(p + o, patches)
        tot_copy(q, q).wait_recv()
        tot_mid[...] += tot_in[q]

    loop(1, patches, add_tot)
    loop(1, visits, lambda o: totz_copy(visit_at(o), v).start())

    def gather(r):
        core_copy(k, r).wait_recv()
        mine[...] = part[k, c, span(r)].astype(jnp.float32) + half[k, span(r)].astype(jnp.float32)

        def one(o):
            j = chip_at(o)
            chip_copy(j, j, r).wait_recv()
            mine[...] += inbox[j, span(r)].astype(jnp.float32)

        loop(1, chips, one)

    def send_lane(i):
        r = visit_at(i)
        gather(r)
        lane_sum[r] = mine[...].astype(jnp.bfloat16)
        lane_copy(r, v).start()

    loop(1, visits, send_lane)
    gather(v)
    tot_z[v] = tot_mid[...]

    def add_lane(o):
        u = visit_at(o)
        lane_copy(u, u).wait_recv()
        mine[...] += lane_in[u].astype(jnp.float32)
        totz_copy(u, u).wait_recv()
        tot_z[v] += tot_z[u]

    loop(1, visits, add_lane)
    coadd[p, span(v)] = (mine[...] / tot_z[v][0:1, 0:1]).astype(jnp.bfloat16)

    loop(1, visits, lambda o: back_copy(visit_at(o), v).start())

    def fan_out(r):
        loop(1, chips, lambda o: fan_copy(chip_at(o), k, r).start())
        pair_copy(k, c, r).start()

    def forward(r):
        def one(o):
            j = chip_at(o)
            fan_copy(j, j, r).wait_recv()
            pair_copy(j, c, r).start()

        loop(1, chips, one)

    fan_out(v)

    def relay(i):
        r = visit_at(i)
        back_copy(r, r).wait_recv()
        fan_out(r)
        forward(visit_at(i - 1))

    loop(1, visits, relay)
    own[0] = coadd[p]
    forward(visit_at(visits - 1))

    def finish(i):
        def one(o):
            j = chip_at(o)
            pair_copy(j, 1 - c, i).wait_recv()
            pair_copy(j, c, i).wait_send()
            core_copy(j, i).wait_send()

        def peer(o):
            j = chip_at(o)
            chip_copy(j, k, i).wait_send()
            fan_copy(j, k, i).wait_send()

        loop(0, chips, one)
        loop(1, chips, peer)

    loop(0, visits, finish)

    def finish_visit(o):
        u = visit_at(o)
        lane_copy(u, v).wait_send()
        totz_copy(u, v).wait_send()
        back_copy(u, v).wait_send()

    loop(1, visits, finish_visit)
    loop(1, patches, lambda o: tot_copy(lax.rem(p + o, patches), p).wait_send())


def merge(part, totals, patches, visits):
    side = part.shape[1]
    chips = patches // 2
    rows = side // visits
    dma = pltpu.SemaphoreType.DMA
    block = pl.BlockSpec(memory_space=pltpu.VMEM)
    pairs = [dma((chips, visits))] * 2
    return pl.pallas_call(
        functools.partial(merge_kernel, chips, visits),
        in_specs=[block, block],
        out_specs=[block, block],
        out_shape=[
            jax.ShapeDtypeStruct((patches, side, side), jnp.bfloat16),
            jax.ShapeDtypeStruct((1, side, side), jnp.bfloat16),
        ],
        scratch_shapes=[
            pltpu.VMEM((chips, side, side), jnp.bfloat16),
            pltpu.VMEM((chips, side, side), jnp.bfloat16),
            pltpu.VMEM((chips, side, side), jnp.bfloat16),
            pltpu.VMEM((visits, rows, side), jnp.bfloat16),
            pltpu.VMEM((visits, rows, side), jnp.bfloat16),
            pltpu.VMEM((rows, side), jnp.float32),
            pltpu.VMEM((patches, 8, 128), jnp.float32),
            pltpu.VMEM((8, 128), jnp.float32),
            pltpu.VMEM((visits, 8, 128), jnp.float32),
        ] + pairs + pairs + [dma((visits,))] * 4 + pairs + pairs + [dma((patches,))] * 2 + [dma((visits,))] * 2,
        compiler_params=pltpu.CompilerParams(collective_id=0, has_side_effects=True),
        name="merge",
    )(part.reshape(chips, 2, side, side), totals)


def local(warped_tiles, tile_weights, kernel_taps, patch_routes):
    patches = lax.axis_size("patch")
    side = warped_tiles.shape[1]
    routes = patch_routes[:, 0]
    weights = tile_weights.astype(jnp.float32)
    rings = ring_rows(kernel_taps)
    part, totals = local_sums(warped_tiles, weights, routes, patches, 64, jnp.bfloat16)
    coadd, coadd_image = merge(part, totals, patches, lax.axis_size("visit"))
    difference = subtract(warped_tiles, rings, routes, coadd, 4)
    return (difference, coadd_image)


def solution(mesh):
    in_specs = (
        P(("visit", "patch"), None, None),
        P(("visit", "patch")),
        P(("visit", "patch"), None, None),
        P(("visit", "patch"), None),
    )
    out_specs = (P(("visit", "patch"), None, None), P("patch", None, None))
    return jax.shard_map(local, mesh=mesh, in_specs=in_specs, out_specs=out_specs, check_vma=False)
```
